256 devices in a mesh: req: 32 (over y, z), head: 8 (over x, core).
Axes of the slice: x: 4, y: 4, z: 8, core: 2. Of those that a mesh axis runs over, the one named last changes fastest.
Arguments:
- tokens: bfloat16 [256, 1024], P('req'), may hold values from -6 to 6
- lengths: int32 [256], P('req'), may hold values from 1 to 512, as said below
- slot_owner: int32 [256], P('req'), may hold values from 0 to 255, as said below
- positions: int32 [256], P('req'), may hold values from 0 to 8191
- variates: int32 [256], P('req'), may hold values from 0 to 7
- cache_variates: int32 [256, 512], P('req'), may hold values from 0 to 7
- kv_cache: bfloat16 [2, 2, 256, 512, 1024], P(None, None, 'req', None, 'head'), may hold values from -6 to 6
- attn_gain: float32 [2, 1024], replicated, may hold values from 0.1 to 1.9
- ffn_gain: float32 [2, 1024], replicated, may hold values from 0.1 to 1.9
- qkv_weight: bfloat16 [2, 1024, 3072], P(None, None, 'head'), may hold values from -0.1875 to 0.1875
- out_weight: bfloat16 [2, 1024, 1024], P(None, 'head'), may hold values from -0.1875 to 0.1875
- gate_up_weight: bfloat16 [2, 2, 1024, 4096], P(None, None, None, 'head'), may hold values from -0.1875 to 0.1875
- down_weight: bfloat16 [2, 4096, 1024], P(None, 'head'), may hold values from -0.09375 to 0.09375
- variate_bias: float32 [2, 2, 16], P(None, None, 'head'), may hold values from -2 to 300
Outputs:
- next_states: bfloat16 [256, 1024], P(('req', 'head'))
The draws below stay inside these ranges and needn't reach their ends.
Inputs may be any that keep to these rules, and one draw needn't show every extreme that they name: `lengths`: live cache positions of each request; the largest is exactly 512 in every draw. `slot_owner`: each request is held in exactly one slot; taken in an order of non-increasing length, the requests fill slot t of every req index in turn t = 0, 1, ..., the req indices in rising order on even turns and in falling order on odd ones; no two slots of one req index hold requests of the same device of next_states (the same 1 request).
All inputs are finite; a program needn't handle non-finite values.
Results may differ from the reference program's by a relative error of at most 0.02.
Values may be sent and summed in bfloat16 or wider, within the bound.
A program may use at most 64 MiB of HBM per device.

```python
import jax
import jax.numpy as jnp
from jax import lax

D = 1024
HEADS = 16
HD = 64
FF = 4096
LAYERS = 2
REQ_DEV = 8
CAP = 512
VARIATES = 8
REQUESTS = 256
SHARE = 1


def draw_variate_bias(key, part):
    first_key = jax.random.fold_in(key, 0)
    modest = jax.random.uniform(first_key, (LAYERS, 2, HEADS), jnp.float32, -2.0, 2.0)
    return modest


def dealing_plan(key):
    base_key = jax.random.fold_in(key, 17)
    short_key, long_key, pick_key, order_key = jax.random.split(base_key, 4)
    short_len = jax.random.randint(short_key, (REQUESTS,), 1, CAP // 4 + 1)
    long_len = jax.random.randint(long_key, (REQUESTS,), CAP // 2, CAP + 1)
    is_long = jax.random.randint(pick_key, (REQUESTS,), 0, 64) == 0
    values = jnp.where(is_long, long_len, short_len).astype(jnp.int32)
    values = values.at[0].set(CAP)
    ordered = -jnp.sort(-values)
    groups = REQUESTS // REQ_DEV
    owner_devices = REQUESTS // SHARE
    device_order = jax.random.permutation(order_key, owner_devices).astype(jnp.int32)
    rank = jnp.arange(REQUESTS, dtype=jnp.int32)
    turn = rank // groups
    place = rank % groups
    per_turn = groups // SHARE
    device_of_rank = device_order[turn * per_turn + place // SHARE]
    request_of_rank = device_of_rank * SHARE + place % SHARE
    group_of_rank = jnp.where(turn % 2 == 0, place, groups - 1 - place)
    slot_of_rank = group_of_rank * REQ_DEV + turn
    lengths_out = jnp.zeros((REQUESTS,), jnp.int32).at[request_of_rank].set(ordered)
    owners_out = jnp.zeros((REQUESTS,), jnp.int32).at[slot_of_rank].set(request_of_rank)
    return (lengths_out, owners_out)


def draw_lengths(key, part):
    return dealing_plan(key)[0]


def draw_slot_owner(key, part):
    return dealing_plan(key)[1]


def touch_ends(result, stream_key, smallest, high):
    spot = [jax.random.randint(jax.random.fold_in(stream_key, axis), (), 0, length) for axis, length in enumerate(result.shape)]
    widest = result.shape.index(max(result.shape))
    next_to = spot[:widest] + [(spot[widest] + 1) % result.shape[widest]] + spot[widest + 1:]
    return result.at[tuple(spot)].set(smallest).at[tuple(next_to)].set(high)


def levels(stream_key, dims, shards, low, largest):
    level = 1.0
    for axis_at, blocks in shards:
        heights = jax.random.uniform(jax.random.fold_in(jax.random.fold_in(stream_key, 6), axis_at), (blocks,), jnp.float32, low / len(shards), largest / len(shards))
        level = level * jnp.repeat(jnp.exp(heights), dims[axis_at] // blocks).reshape((-1,) + (1,) * (len(dims) - 1 - axis_at))
    return level


def bell_draw(rng, extent, width, limit, shards=(), kind=jnp.bfloat16):
    array = width * jax.random.normal(rng, extent, jnp.float32)
    if shards:
        array = array * levels(rng, extent, shards, -0.22, 0.18)
    return jnp.clip(array, -limit, limit).astype(kind)


def setup_inputs(seed: int = 0) -> dict:
    streams_of = jax.random.split(jax.random.key(seed), 15)
    tokens = bell_draw(streams_of[0], (REQUESTS, D), 1.0, 6.0, ((0, 32),))
    lengths = draw_lengths(jax.random.fold_in(streams_of[14], 71), 0)
    slot_owner = draw_slot_owner(jax.random.fold_in(streams_of[14], 71), 0)
    positions = touch_ends(jax.random.randint(streams_of[3], (REQUESTS,), 0, 8192), jax.random.fold_in(streams_of[3], 1), 0, 8191).astype(jnp.int32)
    variates = touch_ends(jax.random.randint(streams_of[4], (REQUESTS,), 0, VARIATES), jax.random.fold_in(streams_of[4], 1), 0, VARIATES - 1).astype(jnp.int32)
    cache_variates = touch_ends(jax.random.randint(streams_of[5], (REQUESTS, CAP), 0, VARIATES), jax.random.fold_in(streams_of[5], 1), 0, VARIATES - 1).astype(jnp.int32)
    kv_cache = bell_draw(streams_of[6], (LAYERS, 2, REQUESTS, CAP, HEADS * HD), 1.0, 6.0, ((2, 32), (4, 8)))
    attn_gain = jnp.clip(1.0 + 0.18 * jax.random.normal(streams_of[7], (LAYERS, D), jnp.float32), 0.1, 1.9)
    ffn_gain = jnp.clip(1.0 + 0.18 * jax.random.normal(streams_of[8], (LAYERS, D), jnp.float32), 0.1, 1.9)
    qkv_weight = bell_draw(streams_of[9], (LAYERS, D, 3 * HEADS * HD), D ** -0.5, 0.1875, ((2, 8),))
    out_weight = bell_draw(streams_of[10], (LAYERS, HEADS * HD, D), (HEADS * HD) ** -0.5, 0.1875, ((1, 8),))
    gate_up_weight = bell_draw(streams_of[11], (LAYERS, 2, D, FF), D ** -0.5, 0.1875, ((3, 8),))
    down_weight = bell_draw(streams_of[12], (LAYERS, FF, D), FF ** -0.5, 0.09375, ((1, 8),))
    variate_bias = draw_variate_bias(jax.random.fold_in(streams_of[14], 71), 0)
    return {"tokens": tokens, "lengths": lengths, "slot_owner": slot_owner, "positions": positions, "variates": variates, "cache_variates": cache_variates, "kv_cache": kv_cache, "attn_gain": attn_gain, "ffn_gain": ffn_gain, "qkv_weight": qkv_weight, "out_weight": out_weight, "gate_up_weight": gate_up_weight, "down_weight": down_weight, "variate_bias": variate_bias}


neg_fill = -1e+30

def rms_scale(stream, gain_row):
    return stream * lax.rsqrt(lax.optimization_barrier(jnp.mean(stream * stream, axis=-1, keepdims=True)) + 1e-06) * gain_row

def rotary(vectors, time_ids):
    half_width = vectors.shape[-1] // 2
    frequency = 10000.0 ** (-2.0 * jnp.arange(half_width, dtype=jnp.float32) / vectors.shape[-1])
    angles = time_ids.astype(jnp.float32)[:, None, None] * frequency[None, None, :]
    cosine = jnp.cos(angles)
    sine_part = jnp.sin(angles)
    front_half = vectors[..., :half_width]
    back_half = vectors[..., half_width:]
    return jnp.concatenate([front_half * cosine - back_half * sine_part, front_half * sine_part + back_half * cosine], axis=-1)

def reference(tokens, lengths, slot_owner, positions, variates, cache_variates, kv_cache, attn_gain, ffn_gain, qkv_weight, out_weight, gate_up_weight, down_weight, variate_bias):
    score_scale = HD ** (-0.5)
    owners = slot_owner
    residual = jnp.take(tokens, owners, axis=0).astype(jnp.float32)
    cache_lengths = jnp.take(lengths, owners)
    time_ids = jnp.take(positions, owners)
    variate_ids = jnp.take(variates, owners)
    for layer_index in range(LAYERS):
        normed = rms_scale(residual, attn_gain[layer_index]).astype(jnp.bfloat16)
        projected = jnp.dot(normed, qkv_weight[layer_index], preferred_element_type=jnp.float32).reshape(REQUESTS, HEADS, 3, HD)
        queries = rotary(projected[:, :, 0], time_ids).astype(jnp.bfloat16)
        key_new = rotary(projected[:, :, 1], time_ids).astype(jnp.bfloat16)
        value_new = projected[:, :, 2].astype(jnp.bfloat16)
        same_bias = variate_bias[layer_index, 0]
        diff_bias = variate_bias[layer_index, 1]

        def one_request(request_items):
            cached_keys, cached_values, cache_var, query_row, key_row, value_row, length_one, variate_one = request_items
            keys_float = cached_keys.reshape(CAP, HEADS, HD).astype(jnp.float32)
            values_float = cached_values.reshape(CAP, HEADS, HD).astype(jnp.float32)
            query_float = query_row.astype(jnp.float32)
            scores = jnp.einsum('hd,chd->hc', query_float, keys_float) * score_scale
            score_bias = jnp.where(cache_var[None, :] == variate_one, same_bias[:, None], diff_bias[:, None])
            scores = scores + score_bias
            live_mask = jnp.arange(CAP, dtype=jnp.int32) < length_one
            scores = jnp.where(live_mask[None, :], scores, neg_fill)
            self_score = lax.optimization_barrier(jnp.sum(query_float * key_row.astype(jnp.float32), axis=-1)) * score_scale + same_bias
            row_top = jnp.maximum(lax.optimization_barrier(jnp.max(scores, axis=1)), self_score)
            weights = jnp.exp(scores - row_top[:, None])
            self_weight = jnp.exp(self_score - row_top)
            denominator = lax.optimization_barrier(jnp.sum(weights, axis=1)) + self_weight
            probs_bf16 = (weights / denominator[:, None]).astype(jnp.bfloat16)
            self_prob = (self_weight / denominator).astype(jnp.bfloat16)
            mixed_heads = jnp.einsum('hc,chd->hd', probs_bf16.astype(jnp.float32), values_float)
            mixed_heads = mixed_heads + self_prob.astype(jnp.float32)[:, None] * value_row.astype(jnp.float32)
            return mixed_heads.reshape(HEADS * HD).astype(jnp.bfloat16)
        attended = lax.map(one_request, (kv_cache[layer_index, 0], kv_cache[layer_index, 1], cache_variates, queries, key_new, value_new, cache_lengths, variate_ids))
        residual = residual + jnp.dot(attended, out_weight[layer_index], preferred_element_type=jnp.float32)
        normed_ffn = rms_scale(residual, ffn_gain[layer_index]).astype(jnp.bfloat16)
        gate_sum = jnp.dot(normed_ffn, gate_up_weight[layer_index, 0], preferred_element_type=jnp.float32)
        up_sum = jnp.dot(normed_ffn, gate_up_weight[layer_index, 1], preferred_element_type=jnp.float32)
        hidden = (jax.nn.silu(gate_sum) * up_sum).astype(jnp.bfloat16)
        residual = residual + jnp.dot(hidden, down_weight[layer_index], preferred_element_type=jnp.float32)
    final_rows = residual.astype(jnp.bfloat16)
    return jnp.zeros_like(final_rows).at[owners].set(final_rows)
```

```python
import functools

import jax
import jax.numpy as jnp
import numpy as np
from jax import lax
from jax.experimental import pallas as pl
from jax.experimental.pallas import tpu as pltpu
from jax.sharding import PartitionSpec as P

HD = 64
LAYERS = 2
LANES = 128
NEG = -1e30
MESH = pl.DeviceIdType.MESH
F32, BF16, I32 = jnp.float32, jnp.bfloat16, jnp.int32


def ring_order(count):
    return sorted(range(count), key=lambda d: -min(d, count - d))


def req_order(y_count, z_count):
    pairs = [(dy, dz) for dy in range(y_count) for dz in range(z_count) if dy or dz]
    return sorted(pairs, key=lambda p: -(min(p[0], y_count - p[0]) + min(p[1], z_count - p[1])))


def head_order(count):
    return sorted(range(1, count), key=lambda d: -min(d // 2, (count - d) // 2))


def iota(shape, axis):
    return lax.broadcasted_iota(I32, shape, axis)


def column(scalars, shape):
    rows = iota(shape, 0) % 8
    out = jnp.zeros(shape, I32)
    for i, s in enumerate(scalars):
        out = jnp.where(rows == i, s, out)
    return out


def rms(stream, gain):
    return stream * lax.rsqrt(jnp.mean(stream * stream, axis=-1, keepdims=True) + 1e-06) * gain


def angles(times, freq):
    lane = iota((8, LANES), 1)
    theta = times.astype(F32) * freq
    sine = jnp.sin(theta)
    return jnp.cos(theta), jnp.where(lane % HD < HD // 2, -sine, sine)


def rotate(u, cosine, sine):
    lane = iota((8, LANES), 1)
    partner = jnp.where(lane % HD < HD // 2, pltpu.roll(u, LANES - HD // 2, 1), pltpu.roll(u, HD // 2, 1))
    return u * cosine + partner * sine


def split_qkv(proj, cosine, sine):
    low = iota((8, LANES), 1) < HD
    t0, t1, t2 = proj[:, :128], proj[:, 128:256], proj[:, 256:384]
    q = jnp.where(low, t0, t1)
    k = pltpu.roll(jnp.where(low, t2, t0), HD, 1)
    v = jnp.where(low, t1, t2)
    q = rotate(q, cosine, sine).astype(BF16)
    k = rotate(k, cosine, sine).astype(BF16)
    prod = q.astype(F32) * k.astype(F32)
    s0 = jnp.sum(jnp.where(low, prod, 0.0), axis=1, keepdims=True) * (HD ** -0.5)
    s1 = jnp.sum(jnp.where(low, 0.0, prod), axis=1, keepdims=True) * (HD ** -0.5)
    return q, v.astype(BF16), s0, s1


def kernel(
    nr, nh, ny, nz,
    tok_h, len_h, own_h, pos_h, var_h, cv_h, kv_h, ag_h, fg_h, qkv_h, out_h, gu_h, dn_h, vb_h, fr_h,
    o_ref,
    tok, cv, kv, ag, fg, qkv, outw, gu, dn, vb, freq,
    len_s, own_s, pos_s, var_s,
    qv_send, meta_send, qv_recv, meta_recv, tok_recv, ar, last_send, last_recv,
    load_sem, send1, recv1, sendm, recvm, sendt, recvt, ar_send, ar_recv, send2, recv2,
):
    me_r = lax.axis_index("req")
    me_h = lax.axis_index("head")
    y, z = me_r // nz, me_r % nz
    peers_r = [(((y + dy) % ny) * nz + (z + dz) % nz) for dy, dz in req_order(ny, nz)]
    peers_h = [(me_h + d) % nh for d in head_order(nh)]

    barrier = pltpu.get_barrier_semaphore()
    for r in peers_r:
        pl.semaphore_signal(barrier, inc=1, device_id=(r, me_h), device_id_type=MESH)
    for h in peers_h:
        pl.semaphore_signal(barrier, inc=1, device_id=(me_r, h), device_id_type=MESH)

    loads = []

    def load(src, dst):
        copy = pltpu.make_async_copy(src, dst, load_sem.at[len(loads)])
        copy.start()
        loads.append(copy)
        return copy

    first = [load(tok_h, tok), load(ag_h, ag), load(pos_h, pos_s), load(len_h, len_s), load(var_h, var_s)]
    first.append(load(fr_h, freq))
    first += [load(qkv_h.at[0], qkv.at[0]), load(own_h, own_s)]
    att_in = [[load(vb_h, vb), load(cv_h, cv), load(kv_h.at[0, 0], kv.at[0, 0])]]
    val_in = [[load(kv_h.at[0, 1], kv.at[0, 1])]]
    out_in = [[load(out_h.at[0], outw.at[0])]]
    gu_in = [[load(fg_h, fg), load(gu_h.at[0], gu.at[0])]]
    dn_in = [[load(dn_h.at[0], dn.at[0])]]
    qkv_in = [[], [load(qkv_h.at[1], qkv.at[1])]]
    att_in.append([load(kv_h.at[1, 0], kv.at[1, 0])])
    val_in.append([load(kv_h.at[1, 1], kv.at[1, 1])])
    out_in.append([load(out_h.at[1], outw.at[1])])
    gu_in.append([load(gu_h.at[1], gu.at[1])])
    dn_in.append([load(dn_h.at[1], dn.at[1])])

    def arrive(copies):
        for c in copies:
            c.wait()

    arrive(first)
    lane8 = iota((8, LANES), 1)
    row8 = iota((8, LANES), 0)
    cosine, sine = angles(column([pos_s[i] for i in range(8)], (8, LANES)), freq[...])
    normed = rms(tok[...].astype(F32), ag[0:1, :]).astype(BF16)
    proj = jnp.dot(normed, qkv[0], preferred_element_type=F32)
    q, v, s0, s1 = split_qkv(proj, cosine, sine)
    qv = jnp.concatenate([q, v], axis=0)
    kind = lane8 % 16
    meta = jnp.where(kind == 0, column([len_s[i] for i in range(8)], (8, LANES)).astype(F32), 0.0)
    meta = jnp.where(kind == 1, column([var_s[i] for i in range(8)], (8, LANES)).astype(F32), meta)
    meta = jnp.where(kind == 2, column([pos_s[i] for i in range(8)], (8, LANES)).astype(F32), meta)
    meta = jnp.where(kind == 3, s0, meta)
    meta = jnp.where(kind == 4, s1, meta)
    meta = jnp.sum(jnp.where(lane8 // 16 == row8, meta, 0.0), axis=0, keepdims=True)
    my_cols = pl.ds(pl.multiple_of(me_h * LANES, LANES), LANES)
    qv_send[...] = qv
    meta_send[...] = meta
    qv_recv[me_r] = qv
    meta_recv[me_r] = meta
    tok_recv[me_r] = tok[:, my_cols]

    pl.semaphore_wait(barrier, len(peers_r) + len(peers_h))

    def send(src, dst, s, r, to):
        pltpu.make_async_remote_copy(
            src_ref=src, dst_ref=dst, send_sem=s, recv_sem=r, device_id=to, device_id_type=MESH
        ).start()

    def finish(ref, sem):
        pltpu.make_async_copy(ref, ref, sem).wait()

    for r in peers_r:
        send(qv_send, qv_recv.at[me_r], send1, recv1, (r, me_h))
        send(meta_send, meta_recv.at[me_r], sendm, recvm, (r, me_h))
    for r in peers_r:
        send(tok.at[:, my_cols], tok_recv.at[me_r], sendt, recvt, (r, me_h))

    owners = [own_s[i] for i in range(8)]
    bases = [(o // 8) * 16 + o % 8 for o in owners]
    pick = column(bases, (16, nr * 16)) + jnp.where(iota((16, nr * 16), 0) >= 8, 8, 0)
    pick = jnp.where(iota((16, nr * 16), 1) == pick, 1.0, 0.0).astype(BF16)
    row16 = iota((16, LANES), 0)
    lane16 = iota((16, LANES), 1)
    half16 = (lane16 // HD) == (row16 // 8)
    low8 = lane8 < HD

    others = pl.ds(0, nr - 1)
    arrive(att_in[0])
    finish(qv_recv.at[others], recv1)
    picked = jnp.dot(pick, qv_recv[...].reshape(nr * 16, LANES), preferred_element_type=F32)
    q, v = picked[:8], picked[8:]
    finish(meta_recv.at[others], recvm)
    meta = jnp.zeros((8, LANES), F32)
    for t, o in enumerate(owners):
        meta = jnp.where(row8 == t, meta_recv[o // 8], meta)
    mine = lane8 // 16 == column([o % 8 for o in owners], (8, LANES))
    meta = [
        jnp.sum(jnp.where(mine & (kind == i), meta, 0.0), axis=1, keepdims=True) for i in range(5)
    ]
    length, variate, time = meta[0].astype(I32), meta[1].astype(I32), meta[2]
    s0, s1 = meta[3], meta[4]
    same_var = cv[...] == variate
    live = iota((8, 512), 1) < length
    live = jnp.concatenate([live.astype(F32)] * 2, axis=0) > 0.5

    def attend(layer, q, v, s0, s1):
        q2 = jnp.where(half16, jnp.concatenate([q, q], axis=0), 0.0)
        raw = jnp.zeros((16, 512), F32)
        for p in range(4):
            qp = jnp.concatenate(
                [jnp.where(row16 % 8 == 2 * p + i, q2, 0.0) for i in range(2)], axis=1
            ).astype(BF16)
            kp = jnp.concatenate([kv[layer, 0, 2 * p], kv[layer, 0, 2 * p + 1]], axis=1)
            raw += lax.dot_general(qp, kp, (((1,), (1,)), ((), ())), preferred_element_type=F32)
        table = vb[layer]
        bias = jnp.concatenate(
            [jnp.where(same_var, table[0:1, h : h + 1], table[1:2, h : h + 1]) for h in range(2)], axis=0
        )
        scores = jnp.where(live, raw * (HD ** -0.5) + bias, NEG)
        own = jnp.concatenate([s0 + table[0:1, 0:1], s1 + table[0:1, 1:2]], axis=0)
        top = jnp.maximum(jnp.max(scores, axis=1, keepdims=True), own)
        weights = jnp.exp(scores - top)
        own_weight = jnp.exp(own - top)
        total = jnp.sum(weights, axis=1, keepdims=True) + own_weight
        probs = (weights / total).astype(BF16)
        own_prob = (own_weight / total).astype(BF16).astype(F32)
        arrive(val_in[layer])
        mixed = jnp.zeros((16, LANES), F32)
        for p in range(4):
            vp = jnp.concatenate([kv[layer, 1, 2 * p], kv[layer, 1, 2 * p + 1]], axis=1)
            got = jnp.dot(probs, vp, preferred_element_type=F32)
            mixed = jnp.where(row16 % 8 == 2 * p, got[:, :128], mixed)
            mixed = jnp.where(row16 % 8 == 2 * p + 1, got[:, 128:], mixed)
        mixed = mixed + own_prob * jnp.concatenate([v, v], axis=0)
        att = jnp.where(low8, mixed[:8], mixed[8:]).astype(BF16)
        arrive(out_in[layer])
        return jnp.dot(att, outw[layer], preferred_element_type=F32)

    def reduce(step, partial):
        folded = jnp.concatenate([partial[:, :512], partial[:, 512:]], axis=0).astype(BF16)
        ar[step, me_h] = folded
        for h in peers_h:
            send(ar.at[step, me_h], ar.at[step, me_h], ar_send.at[step], ar_recv.at[step], (me_r, h))
        return lambda: collect(step)

    def collect(step):
        finish(ar.at[step, pl.ds(0, nh - 1)], ar_recv.at[step])
        total = jnp.sum(ar[step].astype(F32), axis=0)
        return jnp.concatenate([total[:8], total[8:]], axis=1)

    def feed_forward(layer, stream):
        arrive(gu_in[layer])
        normed = rms(stream, fg[layer : layer + 1, :]).astype(BF16)
        gate = jnp.dot(normed, gu[layer, 0], preferred_element_type=F32)
        up = jnp.dot(normed, gu[layer, 1], preferred_element_type=F32)
        hidden = (gate / (1.0 + jnp.exp(-gate)) * up).astype(BF16)
        arrive(dn_in[layer])
        return jnp.dot(hidden, dn[layer], preferred_element_type=F32)

    partial = attend(0, q, v, s0, s1)
    finish(tok_recv.at[others], recvt)
    pick_row = iota((8, nr * 8), 1) == column(owners, (8, nr * 8))
    rows = jnp.dot(
        jnp.where(pick_row, 1.0, 0.0).astype(BF16),
        tok_recv[...].reshape(nr * 8, LANES),
        preferred_element_type=F32,
    )
    partial = partial + jnp.where(
        iota(partial.shape, 1) // LANES == me_h, jnp.concatenate([rows] * (partial.shape[1] // LANES), axis=1), 0.0
    )
    done = reduce(0, partial)
    cosine, sine = angles(jnp.broadcast_to(time, (8, LANES)), freq[...])
    stream = done()
    done = reduce(1, feed_forward(0, stream))
    stream = stream + done()

    arrive(qkv_in[1])
    normed = rms(stream, ag[1:2, :]).astype(BF16)
    q, v, s0, s1 = split_qkv(jnp.dot(normed, qkv[1], preferred_element_type=F32), cosine, sine)
    arrive(att_in[1])
    done = reduce(2, attend(1, q.astype(F32), v.astype(F32), s0, s1))
    stream = stream + done()
    done = reduce(3, feed_forward(1, stream))
    owner_lane = jnp.zeros((nr * 8, 64), I32)
    lane64 = iota((nr * 8, 64), 1)
    for t, o in enumerate(owners):
        owner_lane = jnp.where(lane64 % 8 == t, o, owner_lane)
    row_r = iota((nr * 8, 64), 0)
    route = (row_r % 8 == lane64 // 8) & (owner_lane == (row_r // 8) * nh + me_h)
    route = jnp.where(route, 1.0, 0.0).astype(BF16)
    stream = stream + done()
    final = jnp.concatenate([stream[:, c * LANES : (c + 1) * LANES] for c in range(8)], axis=0).astype(BF16)
    routed = jnp.dot(route, final, preferred_element_type=F32)
    last_send[...] = routed.reshape(nr, 8, LANES).astype(BF16)
    for r in peers_r:
        send(last_send.at[r], last_recv.at[me_r], send2, recv2, (r, me_h))
    last_recv[me_r] = last_send[me_r]
    for ref, sem in (
        (qv_recv.at[others], send1),
        (meta_recv.at[others], sendm),
        (tok_recv.at[others], sendt),
        *((ar.at[i, pl.ds(0, nh - 1)], ar_send.at[i]) for i in range(4)),
        (last_recv.at[others], send2),
    ):
        finish(ref, sem)
    finish(last_recv.at[others], recv2)
    row = jnp.sum(last_recv[...].astype(F32), axis=0)
    for c in range(8):
        o_ref[:, c * LANES : (c + 1) * LANES] = row[c : c + 1, :].astype(BF16)


def solution(mesh):
    nr, nh = mesh.shape["req"], mesh.shape["head"]
    nz = min(8, nr)
    ny = nr // nz

    def per_device(*args):
        d = args[0].shape[1]
        vmem = lambda a: pltpu.VMEM(a.shape, a.dtype)
        freq = jnp.asarray(10000.0 ** (-2.0 * (np.arange(LANES)[None] % (HD // 2)) / HD), F32)
        args = (*args, freq)
        tok, lengths, owner, positions, variates, cv, kv, ag, fg, qkv, outw, gu, dn, vb, _ = args
        dma = pltpu.SemaphoreType.DMA
        return pl.pallas_call(
            functools.partial(kernel, nr, nh, ny, nz),
            out_shape=jax.ShapeDtypeStruct((1, d), BF16),
            in_specs=[pl.BlockSpec(memory_space=pl.ANY)] * len(args),
            out_specs=pl.BlockSpec(memory_space=pltpu.VMEM),
            scratch_shapes=[vmem(a) for a in (tok, cv, kv, ag, fg, qkv, outw, gu, dn, vb, freq)]
            + [pltpu.SMEM(a.shape, a.dtype) for a in (lengths, owner, positions, variates)]
            + [
                pltpu.VMEM((16, LANES), BF16),
                pltpu.VMEM((1, LANES), F32),
                pltpu.VMEM((nr, 16, LANES), BF16),
                pltpu.VMEM((nr, 1, LANES), F32),
                pltpu.VMEM((nr, 8, LANES), BF16),
                pltpu.VMEM((4, nh, 16, 512), BF16),
                pltpu.VMEM((nr, 8, LANES), BF16),
                pltpu.VMEM((nr, 8, LANES), BF16),
                dma((22,)),
                dma, dma, dma, dma, dma, dma,
                dma((4,)),
                dma((4,)),
                dma, dma,
            ],
            compiler_params=pltpu.CompilerParams(collective_id=0, has_side_effects=True),
            name="decode",
        )(*args)

    return jax.shard_map(
        per_device,
        mesh=mesh,
        in_specs=(
            P("req", None),
            P("req"),
            P("req"),
            P("req"),
            P("req"),
            P("req", None),
            P(None, None, "req", None, "head"),
            P(),
            P(),
            P(None, None, "head"),
            P(None, "head", None),
            P(None, None, None, "head"),
            P(None, "head", None),
            P(None, None, "head"),
        ),
        out_specs=P(("req", "head"), None),
        check_vma=False,
    )
```
